32 devices in a mesh: rep: 2 (over y), grp: 4 (over z), sub: 4 (over x, core).
Axes of the slice: x: 2, y: 2, z: 4, core: 2. Of those that a mesh axis runs over, the one named last changes fastest.
Arguments:
- embeddings: bfloat16 [8192, 1024], P(('rep', 'grp', 'sub')), parts along dimension 0, may hold values from -6 to 6
- cluster_ids: int32 [8192, 1], P(('rep', 'grp', 'sub')), parts along dimension 0, may hold values from 0 to 3; in each aligned block of 256 rows (0 to 255, 256 to 511, ...) at most 128 rows name the same one
Outputs:
- max_similarity: float32 [8192], P(('rep', 'grp', 'sub')), parts along dimension 0
The draws below stay inside these ranges and needn't reach their ends.
There are 2 independent parts, one for each index of `rep`. The reference program is written for one: setup_inputs(seed, part) draws one part's arguments, and reference() takes and returns one part's arrays. A program takes and returns all parts, laid end to end along the dimension named above; each array names one. Nothing has to cross between parts.
Inputs may be any that keep to these rules, and one draw needn't show every extreme that they name: `cluster_ids`: cluster numbers run from 0 to 3; among the rows of one device no cluster is named by more than 128 rows, and in every draw some cluster is named by exactly 128 rows of some device.
All inputs are finite; a program needn't handle non-finite values.
Results may differ from the reference program's by a relative error of at most 0.0014.
Values may be sent and summed in bfloat16 or wider, within the bound.
A program may use at most 64 MiB of HBM per device.

```python
import math
import jax
import jax.numpy as jnp
import numpy as np
from jax import lax

D = 1024
ROWS_DEV = 256
CAP = 128
CLUSTERS = 4
DOCS = 4096
N_GRP = 4
N_SUB = 4


def shard_levels(key, shape, pieces, smallest, top_value):
    loudness = 1.0
    for axis_at, blocks in pieces:
        heights = jax.random.uniform(jax.random.fold_in(jax.random.fold_in(key, 6), axis_at), (blocks,), jnp.float32, smallest / len(pieces), top_value / len(pieces))
        loudness = loudness * jnp.repeat(jnp.exp(heights), shape[axis_at] // blocks).reshape((-1,) + (1,) * (len(shape) - 1 - axis_at))
    return loudness


def shared_out(key, own, number, rows, number_of, top, reach, lean):
    sequence = jax.random.permutation(key, number_of)
    crowded, common = load_shares(number_of, rows * top, reach, lean, True), load_shares(number_of, rows * top, reach, lean, False)
    places = jnp.arange(number_of)

    def named(sizes, turn):
        used = int((sizes > 0).sum())
        fixed = max(1, used // 4)
        passed = fixed + (places - fixed + turn * (used - fixed)) % max(1, number_of - fixed)
        return jnp.zeros((number_of,), jnp.int32).at[sequence[jnp.where(places < fixed, places, passed)]].set(jnp.asarray(sizes, jnp.int32))

    sizes = jnp.where(number % 4 == 0, named(crowded, number // 4), named(common, number - number // 4 - 1))
    mixed = jax.random.permutation(jax.random.fold_in(own, 3), number_of)
    source_of, sink = mixed[0:number_of // 2 * 2:2], mixed[1:number_of // 2 * 2:2]
    slack = jnp.minimum(sizes[source_of] - 1, reach - sizes[sink]) // 2
    slack = jnp.where((source_of == sequence[0]) | (sink == sequence[0]) | (sizes[sink] == 0), 0, jnp.maximum(slack, 0))
    passed = jax.random.randint(jax.random.fold_in(own, 4), (number_of // 2,), 0, 1 << 20) % (slack + 1)
    sizes = sizes.at[source_of].add(-passed).at[sink].add(passed)
    items = jnp.searchsorted(jnp.cumsum(sizes), jnp.arange(rows * top), side="right").astype(jnp.int32)
    table = items.reshape(top, rows).T
    table = table[jax.random.permutation(jax.random.fold_in(own, 1), rows)]
    turn = jax.random.randint(jax.random.fold_in(own, 2), (rows, 1), 0, top)
    return jnp.take_along_axis(table, (jnp.arange(top)[None, :] + turn) % top, axis=1)


def load_shares(number_of, total, limit, skew, full):
    portions = [(1 << 20) // math.isqrt(grade ** skew) + 1 for grade in range(1, number_of + 1)]
    largest = limit if full else min(limit, max(-(-total // number_of), total * portions[0] // sum(portions)))
    least = 1 if total - largest >= number_of - 1 else 0
    given, surplus = [largest] + [least] * (number_of - 1), total - largest - least * (number_of - 1)
    while surplus > 0:
        candidates = [i for i in range(1, number_of) if given[i] < largest] or [i for i in range(1, number_of) if given[i] < limit]
        mass, remaining = sum([portions[i] for i in candidates]), surplus
        for i in candidates:
            more = min(limit - given[i], max(1, remaining * portions[i] // mass), surplus)
            given[i] = given[i] + more
            surplus = surplus - more
    return np.array(given)


def centred(own_key, dims, width, reach, split=(), kind=jnp.bfloat16):
    loudness = shard_levels(own_key, dims, split, -0.22, 0.18) if split else 1.0
    result = jax.random.normal(own_key, dims, jnp.float32) * width * loudness
    return jnp.minimum(jnp.maximum(result, -reach), reach).astype(kind)


def setup_inputs(seed: int = 0, part: int = 0) -> dict:
    key_list = jax.random.split(jax.random.key(seed), 3)
    part_splits = jax.random.split(jax.random.fold_in(key_list[2], part), 3)
    embeddings = centred(part_splits[0], (DOCS, D), 1.0, 6.0, ((0, 16),))
    cluster_ids_keys = jax.random.split(jax.random.fold_in(part_splits[1], 1), DOCS // ROWS_DEV)
    cluster_ids_turns = jax.random.permutation(jax.random.fold_in(part_splits[1], 3), DOCS // ROWS_DEV)
    cluster_ids = jax.vmap(lambda own, number: shared_out(jax.random.fold_in(part_splits[1], 2), own, number, ROWS_DEV, CLUSTERS, 1, CAP, 2))(cluster_ids_keys, cluster_ids_turns).reshape((DOCS, 1))
    return dict(embeddings=embeddings, cluster_ids=cluster_ids)


def reference(embeddings, cluster_ids):
    floats = embeddings.astype(jnp.float32)
    unit_rows = (floats * lax.rsqrt(lax.optimization_barrier(jnp.mean(floats * floats, axis=1, keepdims=True)) + 1e-06) / math.sqrt(D)).astype(jnp.bfloat16)
    labels = cluster_ids[:, 0].astype(jnp.int32)
    doc_total = labels.shape[0]
    ordering = jnp.argsort(labels, stable=True).astype(jnp.int32)
    sorted_labels = labels[ordering]
    tallies = jax.ops.segment_sum(jnp.ones_like(labels), labels, CLUSTERS).astype(jnp.int32)
    offsets = (jnp.cumsum(tallies) - tallies).astype(jnp.int32)
    within = (jnp.arange(doc_total, dtype=jnp.int32) - offsets[sorted_labels]).astype(jnp.int32)
    longest = CAP * N_GRP * N_SUB
    packed = jnp.zeros((CLUSTERS, longest, D), embeddings.dtype).at[sorted_labels, within].set(unit_rows[ordering])
    occupied = jnp.zeros((CLUSTERS, longest), jnp.int32).at[sorted_labels, within].set(1)
    diagonal_mask = jnp.eye(longest, dtype=bool)

    def cluster_maxima(pair):
        members, present = pair
        values = members.astype(jnp.float32)
        similar = jnp.dot(values, values.T, precision=lax.Precision.HIGHEST, preferred_element_type=jnp.float32)
        allowed = (present[None, :] > 0) & jnp.logical_not(diagonal_mask)
        return lax.optimization_barrier(jnp.max(jnp.where(allowed, similar, jnp.float32(-1.0)), axis=1))
    highest = lax.map(cluster_maxima, (packed, occupied))
    picked = highest[sorted_labels, within]
    return jnp.zeros((doc_total,), jnp.float32).at[ordering].set(picked)
```

```python
import functools
import math

import jax
import jax.numpy as jnp
from jax import lax
from jax.experimental import pallas as pl
from jax.experimental.pallas import tpu as pltpu
from jax.sharding import PartitionSpec as P

LANES = 128
SUBLANES = 8
VMEM_BUDGET = 24 << 20
MESH = pl.DeviceIdType.MESH


def from_behind(value, axis, by):
    peers = lax.axis_size(axis)
    return lax.ppermute(value, axis, [(i, (i + by) % peers) for i in range(peers)])


def masked_maxima(left_rows, right_rows, right_present, excluded):
    similar = jnp.dot(left_rows, right_rows.T, preferred_element_type=jnp.float32)
    allowed = (right_present[None, :] > 0) & jnp.logical_not(excluded)
    return jnp.where(allowed, similar, jnp.float32(-1.0))


def unit_of(rows, features):
    floats = rows.astype(jnp.float32)
    return (
        floats
        * lax.rsqrt(jnp.mean(floats * floats, axis=1, keepdims=True) + 1e-06)
        / math.sqrt(features)
    ).astype(jnp.bfloat16)


def by_owner(embeddings, cluster_ids):
    rows_dev, features = embeddings.shape
    groups = lax.axis_size("grp")
    subgroup = lax.axis_size("sub")
    capacity = 2 * rows_dev // groups
    unit_rows = unit_of(embeddings, features)
    labels = cluster_ids[:, 0]
    member_table = (labels[:, None] == jnp.arange(groups, dtype=jnp.int32)[None, :]).astype(
        jnp.int32
    )
    running = jnp.cumsum(member_table, axis=0)
    within = jnp.sum(jnp.where(member_table > 0, running - 1, 0), axis=1)
    slot_index = labels * capacity + within
    outgoing = jnp.zeros((groups * capacity, features), jnp.bfloat16).at[slot_index].set(unit_rows)
    occupied = jnp.zeros((groups * capacity,), jnp.int32).at[slot_index].set(1)
    arrived, arrived_present = (
        lax.all_to_all(
            outgoing.reshape(groups, capacity, features),
            "grp",
            split_axis=0,
            concat_axis=0,
            tiled=True,
        ),
        lax.all_to_all(
            occupied.reshape(groups, capacity), "grp", split_axis=0, concat_axis=0, tiled=True
        ),
    )
    owned_rows = arrived.reshape(groups * capacity, features)
    present = arrived_present.reshape(groups * capacity)
    held = owned_rows.shape[0]
    positions = jnp.arange(held, dtype=jnp.int32)
    excluded = positions[:, None] == positions[None, :]
    highest = jnp.max(masked_maxima(owned_rows, owned_rows, present, excluded), axis=1)
    no_exclusion = jnp.zeros((held, held), dtype=bool)
    for offset in range(1, subgroup // 2 + 1):
        peer_rows, peer_present = from_behind((owned_rows, present), "sub", offset)
        scores = masked_maxima(owned_rows, peer_rows, peer_present, no_exclusion)
        highest = jnp.maximum(highest, jnp.max(scores, axis=1))
        if 2 * offset != subgroup:
            column_best = jnp.max(
                jnp.where(present[:, None] > 0, scores, jnp.float32(-1.0)), axis=0
            )
            returned_best = from_behind(column_best, "sub", -offset)
            highest = jnp.maximum(highest, returned_best)
    returned = lax.all_to_all(
        highest.reshape(groups, capacity), "grp", split_axis=0, concat_axis=0, tiled=True
    )
    return returned.reshape(groups * capacity)[slot_index]


def meet_kernel(
    groups, subgroup, chunks,
    emb_ref, ids_ref, out_ref,
    level, foreign, lane_ids, level_ids, ids_col, row_part, col_part,
    ret_out, ret_in, col_out, col_in,
    ids_send, ids_recv, lid_send, lid_recv, lvl_send, lvl_recv, fwd_send,
    z_send, z_recv, ret_send, ret_recv, col_send, col_recv,
):
    rows, features = emb_ref.shape
    size = rows // chunks
    pivot = groups // 2
    z = lax.axis_index("grp")
    s = lax.axis_index("sub")
    partner = s + 1 - 2 * lax.rem(s, 2)
    others = subgroup // 2

    def peer(k):
        return lax.rem(s + k, subgroup)

    def lane(k):
        return lax.rem(z + k, groups)

    barrier = pltpu.get_barrier_semaphore()
    for k in range(1, subgroup):
        pl.semaphore_signal(barrier, 1, device_id={"sub": peer(k)}, device_id_type=MESH)
    for k in range(1, groups):
        pl.semaphore_signal(barrier, 1, device_id={"grp": lane(k)}, device_id_type=MESH)

    def slot(b):
        return pl.ds(pl.multiple_of(b * rows, rows), rows)

    def piece(b, k):
        return pl.ds(pl.multiple_of(b * rows + k * size, size), size)

    def part(k):
        return pl.ds(pl.multiple_of(k * size, size), size)

    def normalize(k, carry):
        level[piece(s, k), :] = unit_of(emb_ref[part(k), :], features)
        return carry

    lax.fori_loop(0, chunks, normalize, 0)
    level_ids[s] = ids_ref[...]
    lane_ids[z] = ids_ref[...]
    col_part[...] = jnp.full(col_part.shape, -1.0, jnp.float32)
    pl.semaphore_wait(barrier, subgroup + groups - 2)

    def remote(src, dst, send, recv, where):
        return pltpu.make_async_remote_copy(
            src_ref=src, dst_ref=dst, send_sem=send, recv_sem=recv,
            device_id=where, device_id_type=MESH,
        )

    def level_ids_copy(k, owner):
        return remote(ids_ref, level_ids.at[owner], lid_send.at[k], lid_recv.at[owner], {"sub": peer(k)})

    def lane_ids_copy(k, owner):
        return remote(ids_ref, lane_ids.at[owner], ids_send.at[k], ids_recv.at[owner], {"grp": lane(k)})

    def own_to_lane(k, where):
        return remote(
            level.at[piece(s, k), :], foreign.at[z, part(k), :], z_send.at[z, k], z_recv.at[z, k],
            {"grp": where},
        )

    def passed_on(i, k, where):
        block = foreign.at[i, part(k), :]
        return remote(block, block, z_send.at[i, k], z_recv.at[i, k], {"grp": where})

    def block_to_peer(owner, send, where):
        block = level.at[slot(owner), :]
        return remote(block, block, send, lvl_recv.at[owner], {"sub": where})

    for k in range(1, groups):
        lane_ids_copy(k, z).start()
    for k in range(1, subgroup):
        level_ids_copy(k, s).start()

    sends_right = z < pivot
    sends_left = z > pivot

    @pl.when(sends_right)
    def _():
        lax.fori_loop(0, chunks, lambda k, c: (own_to_lane(k, z + 1).start(), c)[1], 0)

    @pl.when(sends_left)
    def _():
        lax.fori_loop(0, chunks, lambda k, c: (own_to_lane(k, z - 1).start(), c)[1], 0)

    for k in range(1, others):
        block_to_peer(s, lvl_send.at[k], peer(2 * k)).start()
    block_to_peer(s, lvl_send.at[0], partner).start()

    def visits(i):
        return z > i if i < pivot else (z >= pivot) & (z < i)

    def passes(i):
        return (z > i) & (z < groups - 1) if i < pivot else (z > pivot) & (z < i)

    def onward(i):
        return z + 1 if i < pivot else z - 1

    def take(i, k):
        passed_on(i, k, z).wait_recv()

        @pl.when(passes(i))
        def _():
            passed_on(i, k, onward(i)).start()

    early = list(range(pivot - 1, 0, -1)) + list(range(pivot + 1, groups))
    for i in early + [0]:
        @pl.when(visits(i) if i else z == 1)
        def _(i=i):
            lax.fori_loop(0, chunks, lambda k, c: (take(i, k), c)[1], 0)

    for k in range(1, others):
        came_from = peer(2 * k)
        block_to_peer(came_from, lvl_send.at[0], s).wait_recv()
        block_to_peer(came_from, fwd_send.at[k], partner).start()
    for k in range(0, others):
        came_from = lax.rem(partner + 2 * k, subgroup)
        block_to_peer(came_from, lvl_send.at[0], s).wait_recv()

    for k in range(1, groups):
        lane_ids_copy(k, lane(k)).wait_recv()
    for k in range(1, subgroup):
        level_ids_copy(k, peer(k)).wait_recv()
    for i in range(groups):
        ids_col[i] = jnp.broadcast_to(lane_ids[i], (LANES, rows)).T

    width = subgroup * rows

    def meet(lines, own_ids, shift, store_row, keep_columns):
        similar = lax.dot_general(
            lines, level[...], (((1,), (1,)), ((), ())), preferred_element_type=jnp.float32
        )
        best = jnp.full((size, LANES), -1.0, jnp.float32)
        for at in range(0, width, LANES):
            ids_at = level_ids[at // rows, :, at % rows : at % rows + LANES]
            same = own_ids == ids_at
            if shift is not None:
                across = lax.broadcasted_iota(jnp.int32, (size, LANES), 1) + at
                down = lax.broadcasted_iota(jnp.int32, (size, LANES), 0) + shift
                same = same & (across != down)
            kept = jnp.where(same, similar[:, at : at + LANES], jnp.float32(-1.0))
            best = jnp.maximum(best, kept)
            if keep_columns:
                columns = jnp.max(kept.reshape(size // SUBLANES, SUBLANES, LANES), axis=0)
                col_part[:, at : at + LANES] = jnp.maximum(col_part[:, at : at + LANES], columns)
        store_row(best)

    def meet_foreign(i, k):
        def store(best):
            row_part[i, part(k), :] = best

        meet(foreign[i, part(k), :], ids_col[i, part(k), :], None, store, True)

    def step(k, carry):
        def store(best):
            row_part[z, part(k), :] = best

        meet(level[piece(s, k), :], ids_col[z, part(k), :], s * rows + k * size, store, False)
        for i in early:
            @pl.when(visits(i))
            def _(i=i):
                meet_foreign(i, k)

        @pl.when(z > 1)
        def _():
            take(0, k)

        @pl.when(z > 0)
        def _():
            meet_foreign(0, k)

        return carry

    lax.fori_loop(0, chunks, step, 0)

    def flat(i):
        return jnp.max(row_part[i].T, axis=0, keepdims=True)

    def ret_copy(i, owner, where):
        return remote(ret_out.at[i], ret_in.at[owner], ret_send.at[i], ret_recv.at[owner], {"grp": where})

    def col_copy(k, owner):
        return remote(col_out.at[peer(k)], col_in.at[owner], col_send.at[k], col_recv.at[owner], {"sub": peer(k)})

    for i in [0] + early:
        @pl.when(visits(i))
        def _(i=i):
            ret_out[i] = flat(i)

    for b in range(subgroup):
        col_out[b] = jnp.max(col_part[:, b * rows : (b + 1) * rows], axis=0, keepdims=True)
    for i in [0] + early:
        @pl.when(visits(i))
        def _(i=i):
            ret_copy(i, z, i).start()
    for k in range(1, subgroup):
        col_copy(k, s).start()

    out_ref[...] = jnp.maximum(flat(z), col_out[s])
    for k in range(1, subgroup):
        col_copy(k, peer(k)).wait_recv()
        out_ref[...] = jnp.maximum(out_ref[...], col_in[peer(k)])
    for j in range(1, groups):
        @pl.when((z < j) & (z < pivot) | (z > j) & (z > pivot) & (j >= pivot))
        def _(j=j):
            ret_copy(0, j, z).wait_recv()
            out_ref[...] = jnp.maximum(out_ref[...], ret_in[j])

    for k in range(1, groups):
        lane_ids_copy(k, z).wait_send()
    for k in range(1, subgroup):
        level_ids_copy(k, s).wait_send()
        col_copy(k, s).wait_send()
    for k in range(1, others):
        block_to_peer(s, lvl_send.at[k], peer(2 * k)).wait_send()
        block_to_peer(peer(2 * k), fwd_send.at[k], partner).wait_send()
    block_to_peer(s, lvl_send.at[0], partner).wait_send()

    @pl.when(sends_right | sends_left)
    def _():
        lax.fori_loop(0, chunks, lambda k, c: (own_to_lane(k, z).wait_send(), c)[1], 0)

    for i in [0] + early:
        @pl.when(passes(i))
        def _(i=i):
            lax.fori_loop(0, chunks, lambda k, c: (passed_on(i, k, z).wait_send(), c)[1], 0)

        @pl.when(visits(i))
        def _(i=i):
            ret_copy(i, z, i).wait_send()


def by_meeting(embeddings, cluster_ids, chunks):
    rows, features = embeddings.shape
    groups = lax.axis_size("grp")
    subgroup = lax.axis_size("sub")
    dma = pltpu.SemaphoreType.DMA
    best = pl.pallas_call(
        functools.partial(meet_kernel, groups, subgroup, chunks),
        out_shape=jax.ShapeDtypeStruct((1, rows), jnp.float32),
        in_specs=[pl.BlockSpec(memory_space=pltpu.VMEM)] * 2,
        out_specs=pl.BlockSpec(memory_space=pltpu.VMEM),
        scratch_shapes=[
            pltpu.VMEM((subgroup * rows, features), jnp.bfloat16),
            pltpu.VMEM((groups, rows, features), jnp.bfloat16),
            pltpu.VMEM((groups, 1, rows), jnp.int32),
            pltpu.VMEM((subgroup, 1, rows), jnp.int32),
            pltpu.VMEM((groups, rows, LANES), jnp.int32),
            pltpu.VMEM((groups, rows, LANES), jnp.float32),
            pltpu.VMEM((SUBLANES, subgroup * rows), jnp.float32),
            pltpu.VMEM((groups, 1, rows), jnp.float32),
            pltpu.VMEM((groups, 1, rows), jnp.float32),
            pltpu.VMEM((subgroup, 1, rows), jnp.float32),
            pltpu.VMEM((subgroup, 1, rows), jnp.float32),
            dma((groups,)), dma((groups,)),
            dma((subgroup,)), dma((subgroup,)),
            dma((subgroup,)), dma((subgroup,)), dma((subgroup,)),
            dma((groups, chunks)), dma((groups, chunks)),
            dma((groups,)), dma((groups,)),
            dma((subgroup,)), dma((subgroup,)),
        ],
        compiler_params=pltpu.CompilerParams(collective_id=0, has_side_effects=True),
    )(embeddings, cluster_ids.reshape(1, rows))
    return best.reshape(rows)


def local(embeddings, cluster_ids):
    rows, features = embeddings.shape
    groups = lax.axis_size("grp")
    subgroup = lax.axis_size("sub")
    held = (groups + subgroup) * rows * features * embeddings.dtype.itemsize
    chunks = max(1, rows // 64)
    if held <= VMEM_BUDGET and subgroup % 2 == 0 and groups > 2 and rows % (LANES * 2) == 0:
        return by_meeting(embeddings, cluster_ids, chunks)
    return by_owner(embeddings, cluster_ids)


def solution(mesh):
    return jax.shard_map(
        local,
        mesh=mesh,
        in_specs=(P(("rep", "grp", "sub"), None), P(("rep", "grp", "sub"), None)),
        out_specs=P(("rep", "grp", "sub")),
        check_vma=False,
    )
```

```python
import functools
import math

import jax
import jax.numpy as jnp
from jax import lax
from jax.experimental import pallas as pl
from jax.experimental.pallas import tpu as pltpu
from jax.sharding import PartitionSpec as P

LANES = 128
SUBLANES = 8
VMEM_BUDGET = 24 << 20
MESH = pl.DeviceIdType.MESH


def from_behind(value, axis, by):
    peers = lax.axis_size(axis)
    return lax.ppermute(value, axis, [(i, (i + by) % peers) for i in range(peers)])


def masked_maxima(left_rows, right_rows, right_present, excluded):
    similar = jnp.dot(left_rows, right_rows.T, preferred_element_type=jnp.float32)
    allowed = (right_present[None, :] > 0) & jnp.logical_not(excluded)
    return jnp.where(allowed, similar, jnp.float32(-1.0))


def unit_of(rows, features):
    floats = rows.astype(jnp.float32)
    return (
        floats
        * lax.rsqrt(jnp.mean(floats * floats, axis=1, keepdims=True) + 1e-06)
        / math.sqrt(features)
    ).astype(jnp.bfloat16)


def by_owner(embeddings, cluster_ids):
    rows_dev, features = embeddings.shape
    groups = lax.axis_size("grp")
    subgroup = lax.axis_size("sub")
    capacity = 2 * rows_dev // groups
    unit_rows = unit_of(embeddings, features)
    labels = cluster_ids[:, 0]
    member_table = (labels[:, None] == jnp.arange(groups, dtype=jnp.int32)[None, :]).astype(
        jnp.int32
    )
    running = jnp.cumsum(member_table, axis=0)
    within = jnp.sum(jnp.where(member_table > 0, running - 1, 0), axis=1)
    slot_index = labels * capacity + within
    outgoing = jnp.zeros((groups * capacity, features), jnp.bfloat16).at[slot_index].set(unit_rows)
    occupied = jnp.zeros((groups * capacity,), jnp.int32).at[slot_index].set(1)
    arrived, arrived_present = (
        lax.all_to_all(
            outgoing.reshape(groups, capacity, features),
            "grp",
            split_axis=0,
            concat_axis=0,
            tiled=True,
        ),
        lax.all_to_all(
            occupied.reshape(groups, capacity), "grp", split_axis=0, concat_axis=0, tiled=True
        ),
    )
    owned_rows = arrived.reshape(groups * capacity, features)
    present = arrived_present.reshape(groups * capacity)
    held = owned_rows.shape[0]
    positions = jnp.arange(held, dtype=jnp.int32)
    excluded = positions[:, None] == positions[None, :]
    highest = jnp.max(masked_maxima(owned_rows, owned_rows, present, excluded), axis=1)
    no_exclusion = jnp.zeros((held, held), dtype=bool)
    for offset in range(1, subgroup // 2 + 1):
        peer_rows, peer_present = from_behind((owned_rows, present), "sub", offset)
        scores = masked_maxima(owned_rows, peer_rows, peer_present, no_exclusion)
        highest = jnp.maximum(highest, jnp.max(scores, axis=1))
        if 2 * offset != subgroup:
            column_best = jnp.max(
                jnp.where(present[:, None] > 0, scores, jnp.float32(-1.0)), axis=0
            )
            returned_best = from_behind(column_best, "sub", -offset)
            highest = jnp.maximum(highest, returned_best)
    returned = lax.all_to_all(
        highest.reshape(groups, capacity), "grp", split_axis=0, concat_axis=0, tiled=True
    )
    return returned.reshape(groups * capacity)[slot_index]


def meet_kernel(
    groups, subgroup, chunks,
    emb_ref, ids_ref, out_ref,
    level, foreign, relay, lane_ids, level_ids, ids_col, row_part, col_part,
    ret_out, ret_in, col_out, col_in,
    ids_send, ids_recv, lid_send, lid_recv, lvl_send, lvl_recv, fwd_send,
    z_send, z_recv, out_send, relay_send, relay_recv, ret_send, ret_recv, col_send, col_recv,
):
    rows, features = emb_ref.shape
    size = rows // chunks
    pivot = groups // 2
    rep = lax.axis_index("rep")
    depth = lax.axis_index("grp")
    z = depth * (1 - rep) + (groups - 1 - depth) * rep
    s = lax.axis_index("sub")
    partner = s + 1 - 2 * lax.rem(s, 2)
    others = subgroup // 2
    odd = lax.rem(s, 2) == 1
    even = lax.rem(s, 2) == 0
    relay_at = groups - 1 - z
    across_y = {"rep": 1 - rep}

    def peer(k):
        return lax.rem(s + k, subgroup)

    def lane(k):
        return lax.rem(z + k, groups)

    def at(where):
        return {"grp": where * (1 - rep) + (groups - 1 - where) * rep}

    barrier = pltpu.get_barrier_semaphore()
    for k in range(1, subgroup):
        pl.semaphore_signal(barrier, 1, device_id={"sub": peer(k)}, device_id_type=MESH)
    for k in range(1, groups):
        pl.semaphore_signal(barrier, 1, device_id=at(lane(k)), device_id_type=MESH)

    pl.semaphore_signal(barrier, 1, device_id=across_y, device_id_type=MESH)

    def slot(b):
        return pl.ds(pl.multiple_of(b * rows, rows), rows)

    def piece(b, k):
        return pl.ds(pl.multiple_of(b * rows + k * size, size), size)

    def part(k):
        return pl.ds(pl.multiple_of(k * size, size), size)

    def normalize(k, carry):
        level[piece(s, k), :] = unit_of(emb_ref[part(k), :], features)
        return carry

    lax.fori_loop(0, chunks, normalize, 0)
    level_ids[s] = ids_ref[...]
    lane_ids[z] = ids_ref[...]
    col_part[...] = jnp.full(col_part.shape, -1.0, jnp.float32)
    pl.semaphore_wait(barrier, subgroup + groups - 1)

    def remote(src, dst, send, recv, where):
        return pltpu.make_async_remote_copy(
            src_ref=src, dst_ref=dst, send_sem=send, recv_sem=recv,
            device_id=where, device_id_type=MESH,
        )

    def level_ids_copy(k, owner):
        return remote(ids_ref, level_ids.at[owner], lid_send.at[k], lid_recv.at[owner], {"sub": peer(k)})

    def lane_ids_copy(k, owner):
        return remote(ids_ref, lane_ids.at[owner], ids_send.at[k], ids_recv.at[owner], at(lane(k)))

    def own_to_lane(k, where):
        return remote(
            level.at[piece(s, k), :], foreign.at[z, part(k), :], z_send.at[z, k], z_recv.at[z, k],
            at(where),
        )

    def passed_on(i, k, where):
        block = foreign.at[i, part(k), :]
        return remote(block, block, z_send.at[i, k], z_recv.at[i, k], at(where))

    def own_across(k):
        return remote(
            level.at[piece(s, k), :], relay.at[z, part(k), :], out_send.at[k], relay_recv.at[z, k],
            across_y,
        )

    def relayed(i, k):
        block = relay.at[i, part(k), :]
        return remote(block, block, relay_send.at[i, k], relay_recv.at[i, k], at(z - 1))

    def passed_across(i, k):
        return remote(
            foreign.at[i, part(k), :], relay.at[i, part(k), :], z_send.at[i, k], relay_recv.at[i, k],
            across_y,
        )

    def back_across(i, k):
        return remote(
            relay.at[i, part(k), :], foreign.at[i, part(k), :], relay_send.at[i, k], z_recv.at[i, k],
            across_y,
        )

    def block_to_peer(owner, send, where):
        block = level.at[slot(owner), :]
        return remote(block, block, send, lvl_recv.at[owner], {"sub": where})

    for k in range(1, groups):
        lane_ids_copy(k, z).start()
    for k in range(1, subgroup):
        level_ids_copy(k, s).start()

    at_bank = odd & (z == pivot - 1)
    sends_right = (z < pivot) & (even | (z < pivot - 1))
    sends_left = z > pivot

    @pl.when(at_bank)
    def _():
        lax.fori_loop(0, chunks, lambda k, c: (own_across(k).start(), c)[1], 0)

    @pl.when(sends_right)
    def _():
        lax.fori_loop(0, chunks, lambda k, c: (own_to_lane(k, z + 1).start(), c)[1], 0)

    @pl.when(sends_left)
    def _():
        lax.fori_loop(0, chunks, lambda k, c: (own_to_lane(k, z - 1).start(), c)[1], 0)

    for k in range(1, others):
        block_to_peer(s, lvl_send.at[k], peer(2 * k)).start()
    block_to_peer(s, lvl_send.at[0], partner).start()

    def visits(i):
        return z > i if i < pivot else (z >= pivot) & (z < i)

    turned = lax.rem(s, 2) * (z // (pivot + 1))

    def passes(i):
        if i >= pivot:
            return (z > pivot) & (z < i)
        if i % 2 == 0:
            return (z > i) & (z < groups - 1) & (even | (z < pivot - 1) | (z > pivot - 1))
        return (z > i) & ((even & (z < groups - 1)) | (odd & ((z < pivot - 1) | (z > pivot))))

    def onward(i):
        if i >= pivot:
            return z - 1
        return z + 1 if i % 2 == 0 else z + 1 - 2 * turned

    def take(i):
        def one(k, carry):
            passed_on(i, k, z).wait_recv()

            @pl.when(passes(i))
            def _():
                passed_on(i, k, onward(i)).start()

            return carry

        lax.fori_loop(0, chunks, one, 0)

    last_stop = [pivot if i % 2 == 0 else groups - 1 for i in range(pivot)]

    def relays(i):
        return odd & (relay_at >= pivot - 1) & (relay_at <= last_stop[i])

    def relay_on(i, k):
        @pl.when(relays(i))
        def _():
            relayed(i, k).wait_recv()

            @pl.when(relay_at < last_stop[i])
            def _():
                relayed(i, k).start()

            @pl.when(relay_at == last_stop[i])
            def _():
                back_across(i, k).start()

    for i in range(pivot - 1, -1, -1):
        def relay_step(k, carry, i=i):
            relay_on(i, k)
            if i > 0:
                @pl.when(at_bank)
                def _():
                    passed_on(i - 1, k, z).wait_recv()
                    passed_across(i - 1, k).start()

            return carry

        @pl.when(odd)
        def _(relay_step=relay_step):
            lax.fori_loop(0, chunks, relay_step, 0)

    def soon(i):
        if i >= pivot:
            return visits(i)
        if i % 2 == 0:
            return visits(i) & (z <= pivot)
        return visits(i) & (even | (z < pivot) | (z == groups - 1))

    def later(i):
        if i % 2 == 0:
            return z > pivot
        return odd & (z >= pivot) & (z < groups - 1)

    sources = list(range(pivot - 1, -1, -1)) + list(range(pivot + 1, groups))

    def take_soon(mine):
        for i in sources:
            @pl.when(soon(i) & mine & (even | (z < pivot - 1) | (z > pivot - 1)) if i < pivot else soon(i) & mine)
            def _(i=i):
                take(i)

    take_soon(even)
    for k in range(1, others):
        came_from = peer(2 * k)
        block_to_peer(came_from, lvl_send.at[0], s).wait_recv()
        block_to_peer(came_from, fwd_send.at[k], partner).start()
    for k in range(0, others):
        came_from = lax.rem(partner + 2 * k, subgroup)
        block_to_peer(came_from, lvl_send.at[0], s).wait_recv()

    take_soon(odd)
    for k in range(1, groups):
        lane_ids_copy(k, lane(k)).wait_recv()
    for k in range(1, subgroup):
        level_ids_copy(k, peer(k)).wait_recv()
    for i in range(groups):
        ids_col[i] = jnp.broadcast_to(lane_ids[i], (LANES, rows)).T

    width = subgroup * rows

    def meet(block, i, own):
        similar = lax.dot_general(
            block, level[...], (((1,), (1,)), ((), ())), preferred_element_type=jnp.float32
        )
        own_ids = ids_col[i]
        best = jnp.full((rows, LANES), -1.0, jnp.float32)
        for col in range(0, width, LANES):
            same = own_ids == level_ids[col // rows, :, col % rows : col % rows + LANES]
            if own:
                across = lax.broadcasted_iota(jnp.int32, (rows, LANES), 1) + col
                down = lax.broadcasted_iota(jnp.int32, (rows, LANES), 0) + s * rows
                same = same & (across != down)
            kept = jnp.where(same, similar[:, col : col + LANES], jnp.float32(-1.0))
            best = jnp.maximum(best, kept)
            if not own:
                columns = jnp.max(kept.reshape(rows // SUBLANES, SUBLANES, LANES), axis=0)
                col_part[:, col : col + LANES] = jnp.maximum(col_part[:, col : col + LANES], columns)
        row_part[i] = best

    meet(level[slot(s), :], z, True)
    for i in sources:
        @pl.when(soon(i))
        def _(i=i):
            meet(foreign[i], i, False)

    for i in range(pivot):
        @pl.when(later(i))
        def _(i=i):
            take(i)
            meet(foreign[i], i, False)

    def flat(i):
        return jnp.max(row_part[i].T, axis=0, keepdims=True)

    def ret_copy(i, owner, where):
        return remote(ret_out.at[i], ret_in.at[owner], ret_send.at[i], ret_recv.at[owner], at(where))

    def col_copy(k, owner):
        return remote(col_out.at[peer(k)], col_in.at[owner], col_send.at[k], col_recv.at[owner], {"sub": peer(k)})

    for i in sources:
        @pl.when(visits(i))
        def _(i=i):
            ret_out[i] = flat(i)

    for b in range(subgroup):
        col_out[b] = jnp.max(col_part[:, b * rows : (b + 1) * rows], axis=0, keepdims=True)
    for i in sources:
        @pl.when(visits(i))
        def _(i=i):
            ret_copy(i, z, i).start()
    for k in range(1, subgroup):
        col_copy(k, s).start()

    out_ref[...] = jnp.maximum(flat(z), col_out[s])
    for k in range(1, subgroup):
        col_copy(k, peer(k)).wait_recv()
        out_ref[...] = jnp.maximum(out_ref[...], col_in[peer(k)])
    for j in range(1, groups):
        @pl.when((z < j) & (z < pivot) | (z > j) & (z > pivot) & (j >= pivot))
        def _(j=j):
            ret_copy(0, j, z).wait_recv()
            out_ref[...] = jnp.maximum(out_ref[...], ret_in[j])

    for k in range(1, groups):
        lane_ids_copy(k, z).wait_send()
    for k in range(1, subgroup):
        level_ids_copy(k, s).wait_send()
        col_copy(k, s).wait_send()
    for k in range(1, others):
        block_to_peer(s, lvl_send.at[k], peer(2 * k)).wait_send()
        block_to_peer(peer(2 * k), fwd_send.at[k], partner).wait_send()
    block_to_peer(s, lvl_send.at[0], partner).wait_send()

    @pl.when(at_bank)
    def _():
        lax.fori_loop(0, chunks, lambda k, c: (own_across(k).wait_send(), c)[1], 0)

    for i in range(pivot):
        @pl.when(relays(i))
        def _(i=i):
            lax.fori_loop(0, chunks, lambda k, c: (relayed(i, k).wait_send(), c)[1], 0)

    @pl.when(sends_right | sends_left)
    def _():
        lax.fori_loop(0, chunks, lambda k, c: (own_to_lane(k, z).wait_send(), c)[1], 0)

    for i in sources:
        @pl.when(passes(i))
        def _(i=i):
            lax.fori_loop(0, chunks, lambda k, c: (passed_on(i, k, z).wait_send(), c)[1], 0)

        if i < pivot - 1:
            @pl.when(at_bank)
            def _(i=i):
                lax.fori_loop(0, chunks, lambda k, c: (passed_across(i, k).wait_send(), c)[1], 0)

        @pl.when(visits(i))
        def _(i=i):
            ret_copy(i, z, i).wait_send()


def by_meeting(embeddings, cluster_ids, chunks):
    rows, features = embeddings.shape
    groups = lax.axis_size("grp")
    subgroup = lax.axis_size("sub")
    dma = pltpu.SemaphoreType.DMA
    best = pl.pallas_call(
        functools.partial(meet_kernel, groups, subgroup, chunks),
        out_shape=jax.ShapeDtypeStruct((1, rows), jnp.float32),
        in_specs=[pl.BlockSpec(memory_space=pltpu.VMEM)] * 2,
        out_specs=pl.BlockSpec(memory_space=pltpu.VMEM),
        scratch_shapes=[
            pltpu.VMEM((subgroup * rows, features), jnp.bfloat16),
            pltpu.VMEM((groups, rows, features), jnp.bfloat16),
            pltpu.VMEM((groups // 2, rows, features), jnp.bfloat16),
            pltpu.VMEM((groups, 1, rows), jnp.int32),
            pltpu.VMEM((subgroup, 1, rows), jnp.int32),
            pltpu.VMEM((groups, rows, LANES), jnp.int32),
            pltpu.VMEM((groups, rows, LANES), jnp.float32),
            pltpu.VMEM((SUBLANES, subgroup * rows), jnp.float32),
            pltpu.VMEM((groups, 1, rows), jnp.float32),
            pltpu.VMEM((groups, 1, rows), jnp.float32),
            pltpu.VMEM((subgroup, 1, rows), jnp.float32),
            pltpu.VMEM((subgroup, 1, rows), jnp.float32),
            dma((groups,)), dma((groups,)),
            dma((subgroup,)), dma((subgroup,)),
            dma((subgroup,)), dma((subgroup,)), dma((subgroup,)),
            dma((groups, chunks)), dma((groups, chunks)),
            dma((chunks,)), dma((groups // 2, chunks)), dma((groups // 2, chunks)),
            dma((groups,)), dma((groups,)),
            dma((subgroup,)), dma((subgroup,)),
        ],
        compiler_params=pltpu.CompilerParams(collective_id=0, has_side_effects=True),
    )(embeddings, cluster_ids.reshape(1, rows))
    return best.reshape(rows)


def local(embeddings, cluster_ids):
    rows, features = embeddings.shape
    groups = lax.axis_size("grp")
    subgroup = lax.axis_size("sub")
    held = (groups + subgroup) * rows * features * embeddings.dtype.itemsize
    chunks = max(1, rows // 32)
    paired = lax.axis_size("rep") == 2 and subgroup % 2 == 0 and groups // 2 == 2
    if held <= VMEM_BUDGET and paired and groups % 2 == 0 and rows % (LANES * 2) == 0:
        return by_meeting(embeddings, cluster_ids, chunks)
    return by_owner(embeddings, cluster_ids)


def solution(mesh):
    return jax.shard_map(
        local,
        mesh=mesh,
        in_specs=(P(("rep", "grp", "sub"), None), P(("rep", "grp", "sub"), None)),
        out_specs=P(("rep", "grp", "sub")),
        check_vma=False,
    )
```

```python
import functools
import math

import jax
import jax.numpy as jnp
from jax import lax
from jax.experimental import pallas as pl
from jax.experimental.pallas import tpu as pltpu
from jax.sharding import PartitionSpec as P

LANES = 128
SUBLANES = 8
VMEM_BUDGET = 24 << 20
MESH = pl.DeviceIdType.MESH


def from_behind(value, axis, by):
    peers = lax.axis_size(axis)
    return lax.ppermute(value, axis, [(i, (i + by) % peers) for i in range(peers)])


def masked_maxima(left_rows, right_rows, right_present, excluded):
    similar = jnp.dot(left_rows, right_rows.T, preferred_element_type=jnp.float32)
    allowed = (right_present[None, :] > 0) & jnp.logical_not(excluded)
    return jnp.where(allowed, similar, jnp.float32(-1.0))


def unit_of(rows, features):
    floats = rows.astype(jnp.float32)
    return (
        floats
        * lax.rsqrt(jnp.mean(floats * floats, axis=1, keepdims=True) + 1e-06)
        / math.sqrt(features)
    ).astype(jnp.bfloat16)


def by_owner(embeddings, cluster_ids):
    rows_dev, features = embeddings.shape
    groups = lax.axis_size("grp")
    subgroup = lax.axis_size("sub")
    capacity = 2 * rows_dev // groups
    unit_rows = unit_of(embeddings, features)
    labels = cluster_ids[:, 0]
    member_table = (labels[:, None] == jnp.arange(groups, dtype=jnp.int32)[None, :]).astype(
        jnp.int32
    )
    running = jnp.cumsum(member_table, axis=0)
    within = jnp.sum(jnp.where(member_table > 0, running - 1, 0), axis=1)
    slot_index = labels * capacity + within
    outgoing = jnp.zeros((groups * capacity, features), jnp.bfloat16).at[slot_index].set(unit_rows)
    occupied = jnp.zeros((groups * capacity,), jnp.int32).at[slot_index].set(1)
    arrived, arrived_present = (
        lax.all_to_all(
            outgoing.reshape(groups, capacity, features),
            "grp",
            split_axis=0,
            concat_axis=0,
            tiled=True,
        ),
        lax.all_to_all(
            occupied.reshape(groups, capacity), "grp", split_axis=0, concat_axis=0, tiled=True
        ),
    )
    owned_rows = arrived.reshape(groups * capacity, features)
    present = arrived_present.reshape(groups * capacity)
    held = owned_rows.shape[0]
    positions = jnp.arange(held, dtype=jnp.int32)
    excluded = positions[:, None] == positions[None, :]
    highest = jnp.max(masked_maxima(owned_rows, owned_rows, present, excluded), axis=1)
    no_exclusion = jnp.zeros((held, held), dtype=bool)
    for offset in range(1, subgroup // 2 + 1):
        peer_rows, peer_present = from_behind((owned_rows, present), "sub", offset)
        scores = masked_maxima(owned_rows, peer_rows, peer_present, no_exclusion)
        highest = jnp.maximum(highest, jnp.max(scores, axis=1))
        if 2 * offset != subgroup:
            column_best = jnp.max(
                jnp.where(present[:, None] > 0, scores, jnp.float32(-1.0)), axis=0
            )
            returned_best = from_behind(column_best, "sub", -offset)
            highest = jnp.maximum(highest, returned_best)
    returned = lax.all_to_all(
        highest.reshape(groups, capacity), "grp", split_axis=0, concat_axis=0, tiled=True
    )
    return returned.reshape(groups * capacity)[slot_index]


def meet_kernel(
    groups, subgroup, chunks,
    emb_ref, ids_ref, out_ref,
    level, foreign, relay, lane_ids, level_ids, ids_col, row_part, col_part,
    ret_out, ret_in, col_out, col_in,
    ids_send, ids_recv, lid_send, lid_recv, lvl_send, lvl_recv, fwd_send,
    z_send, z_recv, out_send, relay_send, relay_recv, ret_send, ret_recv, col_send, col_recv,
):
    rows, features = emb_ref.shape
    size = rows // chunks
    pivot = groups // 2
    rep = lax.axis_index("rep")
    depth = lax.axis_index("grp")
    z = depth * (1 - rep) + (groups - 1 - depth) * rep
    s = lax.axis_index("sub")
    partner = s + 1 - 2 * lax.rem(s, 2)
    others = subgroup // 2
    odd = lax.rem(s, 2) == 1
    even = lax.rem(s, 2) == 0
    relay_at = groups - 1 - z
    across_y = {"rep": 1 - rep}

    def peer(k):
        return lax.rem(s + k, subgroup)

    def lane(k):
        return lax.rem(z + k, groups)

    def at(where):
        return {"grp": where * (1 - rep) + (groups - 1 - where) * rep}

    barrier = pltpu.get_barrier_semaphore()
    for k in range(1, subgroup):
        pl.semaphore_signal(barrier, 1, device_id={"sub": peer(k)}, device_id_type=MESH)
    for k in range(1, groups):
        pl.semaphore_signal(barrier, 1, device_id=at(lane(k)), device_id_type=MESH)

    pl.semaphore_signal(barrier, 1, device_id=across_y, device_id_type=MESH)

    def slot(b):
        return pl.ds(pl.multiple_of(b * rows, rows), rows)

    def piece(b, k):
        return pl.ds(pl.multiple_of(b * rows + k * size, size), size)

    def part(k):
        return pl.ds(pl.multiple_of(k * size, size), size)

    def normalize(k, carry):
        level[piece(s, k), :] = unit_of(emb_ref[part(k), :], features)
        return carry

    lax.fori_loop(0, chunks, normalize, 0)
    level_ids[s] = ids_ref[...]
    lane_ids[z] = ids_ref[...]
    col_part[...] = jnp.full(col_part.shape, -1.0, jnp.float32)
    pl.semaphore_wait(barrier, subgroup + groups - 1)

    def remote(src, dst, send, recv, where):
        return pltpu.make_async_remote_copy(
            src_ref=src, dst_ref=dst, send_sem=send, recv_sem=recv,
            device_id=where, device_id_type=MESH,
        )

    def level_ids_copy(k, owner):
        return remote(ids_ref, level_ids.at[owner], lid_send.at[k], lid_recv.at[owner], {"sub": peer(k)})

    def lane_ids_copy(k, owner):
        return remote(ids_ref, lane_ids.at[owner], ids_send.at[k], ids_recv.at[owner], at(lane(k)))

    def own_to_lane(k, where):
        return remote(
            level.at[piece(s, k), :], foreign.at[z, part(k), :], z_send.at[z, k], z_recv.at[z, k],
            at(where),
        )

    def passed_on(i, k, where):
        block = foreign.at[i, part(k), :]
        return remote(block, block, z_send.at[i, k], z_recv.at[i, k], at(where))

    def own_across(k):
        return remote(
            level.at[piece(s, k), :], relay.at[z, part(k), :], out_send.at[k], relay_recv.at[z, k],
            across_y,
        )

    def relayed(i, k):
        block = relay.at[i, part(k), :]
        return remote(block, block, relay_send.at[i, k], relay_recv.at[i, k], at(z - 1))

    def passed_across(i, k):
        return remote(
            foreign.at[i, part(k), :], relay.at[i, part(k), :], z_send.at[i, k], relay_recv.at[i, k],
            across_y,
        )

    def back_across(i, k):
        return remote(
            relay.at[i, part(k), :], foreign.at[i, part(k), :], relay_send.at[i, k], z_recv.at[i, k],
            across_y,
        )

    def block_to_peer(owner, send, where):
        block = level.at[slot(owner), :]
        return remote(block, block, send, lvl_recv.at[owner], {"sub": where})

    for k in range(1, groups):
        lane_ids_copy(k, z).start()
    for k in range(1, subgroup):
        level_ids_copy(k, s).start()

    at_bank = odd & (z == pivot - 1)
    sends_right = (z < pivot) & (even | (z < pivot - 1))
    sends_left = z > pivot

    @pl.when(at_bank)
    def _():
        lax.fori_loop(0, chunks, lambda k, c: (own_across(k).start(), c)[1], 0)

    @pl.when(sends_right)
    def _():
        lax.fori_loop(0, chunks, lambda k, c: (own_to_lane(k, z + 1).start(), c)[1], 0)

    @pl.when(sends_left)
    def _():
        lax.fori_loop(0, chunks, lambda k, c: (own_to_lane(k, z - 1).start(), c)[1], 0)

    for k in range(1, others):
        block_to_peer(s, lvl_send.at[k], peer(2 * k)).start()
    block_to_peer(s, lvl_send.at[0], partner).start()

    def visits(i):
        return z > i if i < pivot else (z >= pivot) & (z < i)

    turned = lax.rem(s, 2) * (z // (pivot + 1))

    def passes(i):
        if i >= pivot:
            return (z > pivot) & (z < i)
        if i % 2 == 0:
            return (z > i) & (z < groups - 1) & (even | (z < pivot - 1) | (z > pivot - 1))
        return (z > i) & ((even & (z < groups - 1)) | (odd & ((z < pivot - 1) | (z > pivot))))

    def onward(i):
        if i >= pivot:
            return z - 1
        return z + 1 if i % 2 == 0 else z + 1 - 2 * turned

    def take_one(i, k):
        passed_on(i, k, z).wait_recv()

        @pl.when(passes(i))
        def _():
            passed_on(i, k, onward(i)).start()

    def take(i, first=0):
        lax.fori_loop(first, chunks, lambda k, c: (take_one(i, k), c)[1], 0)

    lag = chunks // 2
    lagged = odd & (z == pivot)
    last_stop = [pivot if i % 2 == 0 else groups - 1 for i in range(pivot)]

    def relays(i):
        return odd & (relay_at >= pivot - 1) & (relay_at <= last_stop[i])

    def relay_on(i, k):
        @pl.when(relays(i))
        def _():
            relayed(i, k).wait_recv()

            @pl.when(relay_at < last_stop[i])
            def _():
                relayed(i, k).start()

            @pl.when(relay_at == last_stop[i])
            def _():
                back_across(i, k).start()

    for i in range(pivot - 1, -1, -1):
        def relay_step(k, carry, i=i):
            relay_on(i, k)
            if i > 0:
                @pl.when(at_bank)
                def _():
                    passed_on(i - 1, k, z).wait_recv()
                    passed_across(i - 1, k).start()

            else:
                @pl.when(lagged & (k >= lag))
                def _():
                    take_one(0, k - lag)

            return carry

        @pl.when(odd)
        def _(relay_step=relay_step):
            lax.fori_loop(0, chunks, relay_step, 0)

    @pl.when(lagged)
    def _():
        take(0, chunks - lag)

    def soon(i):
        if i >= pivot:
            return visits(i)
        if i % 2 == 0:
            return visits(i) & (z <= pivot)
        return visits(i) & (even | (z < pivot) | (z == groups - 1))

    def later(i):
        if i % 2 == 0:
            return z > pivot
        return odd & (z >= pivot) & (z < groups - 1)

    sources = list(range(pivot - 1, -1, -1)) + list(range(pivot + 1, groups))

    def take_soon(mine):
        for i in sources:
            @pl.when(soon(i) & mine & (even | (z < pivot) | (z > pivot) if i == 0 else z >= 0) & (even | (z < pivot - 1) | (z > pivot - 1)) if i < pivot else soon(i) & mine)
            def _(i=i):
                take(i)

    take_soon(even)
    for k in range(1, others):
        came_from = peer(2 * k)
        block_to_peer(came_from, lvl_send.at[0], s).wait_recv()
        block_to_peer(came_from, fwd_send.at[k], partner).start()
    for k in range(0, others):
        came_from = lax.rem(partner + 2 * k, subgroup)
        block_to_peer(came_from, lvl_send.at[0], s).wait_recv()

    take_soon(odd)
    for k in range(1, groups):
        lane_ids_copy(k, lane(k)).wait_recv()
    for k in range(1, subgroup):
        level_ids_copy(k, peer(k)).wait_recv()
    for i in range(groups):
        ids_col[i] = jnp.broadcast_to(lane_ids[i], (LANES, rows)).T

    width = subgroup * rows

    def meet(block, i, own):
        similar = lax.dot_general(
            block, level[...], (((1,), (1,)), ((), ())), preferred_element_type=jnp.float32
        )
        own_ids = ids_col[i]
        best = jnp.full((rows, LANES), -1.0, jnp.float32)
        for col in range(0, width, LANES):
            same = own_ids == level_ids[col // rows, :, col % rows : col % rows + LANES]
            if own:
                across = lax.broadcasted_iota(jnp.int32, (rows, LANES), 1) + col
                down = lax.broadcasted_iota(jnp.int32, (rows, LANES), 0) + s * rows
                same = same & (across != down)
            kept = jnp.where(same, similar[:, col : col + LANES], jnp.float32(-1.0))
            best = jnp.maximum(best, kept)
            if not own:
                columns = jnp.max(kept.reshape(rows // SUBLANES, SUBLANES, LANES), axis=0)
                col_part[:, col : col + LANES] = jnp.maximum(col_part[:, col : col + LANES], columns)
        row_part[i] = best

    def flat(i):
        return jnp.max(row_part[i].T, axis=0, keepdims=True)

    def ret_copy(i, owner, where):
        return remote(ret_out.at[i], ret_in.at[owner], ret_send.at[i], ret_recv.at[owner], at(where))

    def give_back(i):
        meet(foreign[i], i, False)
        ret_out[i] = flat(i)
        ret_copy(i, z, i).start()

    meet(level[slot(s), :], z, True)
    for i in sources:
        @pl.when(soon(i))
        def _(i=i):
            give_back(i)

    for i in range(pivot):
        @pl.when(later(i))
        def _(i=i):
            take(i)
            give_back(i)

    def col_copy(k, owner):
        return remote(col_out.at[peer(k)], col_in.at[owner], col_send.at[k], col_recv.at[owner], {"sub": peer(k)})

    for b in range(subgroup):
        col_out[b] = jnp.max(col_part[:, b * rows : (b + 1) * rows], axis=0, keepdims=True)
    for k in range(1, subgroup):
        col_copy(k, s).start()

    out_ref[...] = jnp.maximum(flat(z), col_out[s])
    for k in range(1, subgroup):
        col_copy(k, peer(k)).wait_recv()
        out_ref[...] = jnp.maximum(out_ref[...], col_in[peer(k)])
    for j in range(1, groups):
        @pl.when((z < j) & (z < pivot) | (z > j) & (z > pivot) & (j >= pivot))
        def _(j=j):
            ret_copy(0, j, z).wait_recv()
            out_ref[...] = jnp.maximum(out_ref[...], ret_in[j])

    for k in range(1, groups):
        lane_ids_copy(k, z).wait_send()
    for k in range(1, subgroup):
        level_ids_copy(k, s).wait_send()
        col_copy(k, s).wait_send()
    for k in range(1, others):
        block_to_peer(s, lvl_send.at[k], peer(2 * k)).wait_send()
        block_to_peer(peer(2 * k), fwd_send.at[k], partner).wait_send()
    block_to_peer(s, lvl_send.at[0], partner).wait_send()

    @pl.when(at_bank)
    def _():
        lax.fori_loop(0, chunks, lambda k, c: (own_across(k).wait_send(), c)[1], 0)

    for i in range(pivot):
        @pl.when(relays(i))
        def _(i=i):
            lax.fori_loop(0, chunks, lambda k, c: (relayed(i, k).wait_send(), c)[1], 0)

    @pl.when(sends_right | sends_left)
    def _():
        lax.fori_loop(0, chunks, lambda k, c: (own_to_lane(k, z).wait_send(), c)[1], 0)

    for i in sources:
        @pl.when(passes(i))
        def _(i=i):
            lax.fori_loop(0, chunks, lambda k, c: (passed_on(i, k, z).wait_send(), c)[1], 0)

        if i < pivot - 1:
            @pl.when(at_bank)
            def _(i=i):
                lax.fori_loop(0, chunks, lambda k, c: (passed_across(i, k).wait_send(), c)[1], 0)

        @pl.when(visits(i))
        def _(i=i):
            ret_copy(i, z, i).wait_send()


def by_meeting(embeddings, cluster_ids, chunks):
    rows, features = embeddings.shape
    groups = lax.axis_size("grp")
    subgroup = lax.axis_size("sub")
    dma = pltpu.SemaphoreType.DMA
    best = pl.pallas_call(
        functools.partial(meet_kernel, groups, subgroup, chunks),
        out_shape=jax.ShapeDtypeStruct((1, rows), jnp.float32),
        in_specs=[pl.BlockSpec(memory_space=pltpu.VMEM)] * 2,
        out_specs=pl.BlockSpec(memory_space=pltpu.VMEM),
        scratch_shapes=[
            pltpu.VMEM((subgroup * rows, features), jnp.bfloat16),
            pltpu.VMEM((groups, rows, features), jnp.bfloat16),
            pltpu.VMEM((groups // 2, rows, features), jnp.bfloat16),
            pltpu.VMEM((groups, 1, rows), jnp.int32),
            pltpu.VMEM((subgroup, 1, rows), jnp.int32),
            pltpu.VMEM((groups, rows, LANES), jnp.int32),
            pltpu.VMEM((groups, rows, LANES), jnp.float32),
            pltpu.VMEM((SUBLANES, subgroup * rows), jnp.float32),
            pltpu.VMEM((groups, 1, rows), jnp.float32),
            pltpu.VMEM((groups, 1, rows), jnp.float32),
            pltpu.VMEM((subgroup, 1, rows), jnp.float32),
            pltpu.VMEM((subgroup, 1, rows), jnp.float32),
            dma((groups,)), dma((groups,)),
            dma((subgroup,)), dma((subgroup,)),
            dma((subgroup,)), dma((subgroup,)), dma((subgroup,)),
            dma((groups, chunks)), dma((groups, chunks)),
            dma((chunks,)), dma((groups // 2, chunks)), dma((groups // 2, chunks)),
            dma((groups,)), dma((groups,)),
            dma((subgroup,)), dma((subgroup,)),
        ],
        compiler_params=pltpu.CompilerParams(collective_id=0, has_side_effects=True),
    )(embeddings, cluster_ids.reshape(1, rows))
    return best.reshape(rows)


def local(embeddings, cluster_ids):
    rows, features = embeddings.shape
    groups = lax.axis_size("grp")
    subgroup = lax.axis_size("sub")
    held = (groups + subgroup) * rows * features * embeddings.dtype.itemsize
    chunks = max(1, rows // 32)
    paired = lax.axis_size("rep") == 2 and subgroup % 2 == 0 and groups // 2 == 2
    if held <= VMEM_BUDGET and paired and groups % 2 == 0 and rows % (LANES * 2) == 0:
        return by_meeting(embeddings, cluster_ids, chunks)
    return by_owner(embeddings, cluster_ids)


def solution(mesh):
    return jax.shard_map(
        local,
        mesh=mesh,
        in_specs=(P(("rep", "grp", "sub"), None), P(("rep", "grp", "sub"), None)),
        out_specs=P(("rep", "grp", "sub")),
        check_vma=False,
    )
```
